32 devices in a mesh: freq: 2 (over y), space: 16 (over z, x, core).
Axes of the slice: x: 2, y: 2, z: 4, core: 2. Of those that a mesh axis runs over, the one named last changes fastest.
Arguments:
- probes: float32 [2, 32, 128, 128], P(None, 'space'), may hold values from -6 to 6
- background: float32 [2, 2, 32, 128, 128], P('freq', None, 'space'), may hold values from -6 to 6
- medium: float32 [32, 128, 128], P('space'), may hold values from 0.5 to 2
- shifts: float32 [2, 2], P('freq'), may hold values from -1.25 to 1, as said below
- receivers: int32 [32, 128, 128], P('space'), may hold values 0 or 1
Outputs:
- hessian: float32 [2, 32, 128, 128], P(None, 'space', 'freq')
The draws below stay inside these ranges and needn't reach their ends.
Inputs may be any that keep to these rules, and one draw needn't show every extreme that they name: `shifts`: column 0 lies in [-1.25, -0.5], column 1 in [0.2, 1.0].
All inputs are finite; a program needn't handle non-finite values. No bound on the sum of `receivers` on one device may be relied on, other than what follows from the above.
Results may differ from the reference program's by a relative error of at most 0.00002.
Values sent between devices are 32-bit elements; how exact they have to be, the bound alone decides.
A program may use at most 64 MiB of HBM per device.

```python
import math
import jax
import jax.numpy as jnp

NY = 128
NZ = 128
PROBES = 2
STEPS = 4
FREQS = 2
NX = 32


def draw_probes(key, part):
    shape = (PROBES, NX, NY, NZ)
    inner = jax.random.fold_in(key, 11)
    return jnp.clip(jax.random.normal(inner, shape, jnp.float32), -6.0, 6.0)


def draw_background(key, part):
    shape = (FREQS, 2, NX, NY, NZ)
    inner = jax.random.fold_in(key, 23)
    return jnp.clip(jax.random.normal(inner, shape, jnp.float32), -6.0, 6.0)


def draw_shifts(key, part):
    inner = jax.random.fold_in(key, 37)
    real_part = jax.random.uniform(jax.random.fold_in(inner, 1), (FREQS, 1), jnp.float32, -1.25, -0.5)
    imag_part = jax.random.uniform(jax.random.fold_in(inner, 2), (FREQS, 1), jnp.float32, 0.2, 1.0)
    return jnp.concatenate([real_part, imag_part], axis=1)


def plant(values, stream_key, least, largest):
    longest = values.shape.index(max(values.shape))
    spots = []
    for shift in (0, 1):
        where = [jax.random.randint(jax.random.fold_in(stream_key, axis), (), 0, length) for axis, length in enumerate(values.shape)]
        where[longest] = (where[longest] + shift) % values.shape[longest]
        spots.append(tuple(where))
    return values.at[spots[0]].set(least).at[spots[1]].set(largest)


def levels(key, shape, split, smallest, high):
    gain = 1.0
    for position, blocks in split:
        steps = jax.random.uniform(jax.random.fold_in(jax.random.fold_in(key, 6), position), (blocks,), jnp.float32, smallest / len(split), high / len(split))
        gain = gain * jnp.repeat(jnp.exp(steps), shape[position] // blocks).reshape((-1,) + (1,) * (len(shape) - 1 - position))
    return gain


def setup_inputs(seed: int = 0) -> dict:
    key_of = jax.random.split(jax.random.key(seed), 6)
    probes = draw_probes(jax.random.fold_in(key_of[5], 71), 0)
    background = draw_background(jax.random.fold_in(key_of[5], 71), 0)
    medium = jnp.clip(jnp.exp(math.log(2.0) - 1.3862944 * jax.random.uniform(key_of[2], (NX, NY, NZ), jnp.float32) ** levels(key_of[2], (NX, NY, NZ), ((0, 16),), -0.2, 0.2)), 0.5, 2.0)
    shifts = draw_shifts(jax.random.fold_in(key_of[5], 71), 0)
    receivers = plant((jax.random.randint(key_of[4], (NX, NY, NZ), 0, 4) < 3).astype(jnp.int32), jax.random.fold_in(key_of[4], 1), 0, 1)
    return dict(probes=probes, background=background, medium=medium, shifts=shifts, receivers=receivers)


OMEGA_RELAX = 0.8


def neighbours(extended):
    center = extended[:, :, 1:-1]
    beside_all = extended[:, :, 2:] + extended[:, :, :-2]
    pad_y_low = ((0, 0), (0, 0), (0, 0), (0, 1), (0, 0))
    pad_y_high = ((0, 0), (0, 0), (0, 0), (1, 0), (0, 0))
    pad_z_low = ((0, 0), (0, 0), (0, 0), (0, 0), (0, 1))
    pad_z_high = ((0, 0), (0, 0), (0, 0), (0, 0), (1, 0))
    beside_all = beside_all + jnp.pad(center[:, :, :, 1:], pad_y_low) + jnp.pad(center[:, :, :, :-1], pad_y_high)
    beside_all = beside_all + jnp.pad(center[:, :, :, :, 1:], pad_z_low) + jnp.pad(center[:, :, :, :, :-1], pad_z_high)
    return center, beside_all


def sweep_once(extended, factors, source):
    diag_re, diag_im, inv_re, inv_im = factors
    center, beside_all = neighbours(extended)
    resid_re = source[0] - (diag_re * center[0] - diag_im * center[1]) + beside_all[0]
    resid_im = source[1] - (diag_re * center[1] + diag_im * center[0]) + beside_all[1]
    return center + jnp.stack([inv_re * resid_re - inv_im * resid_im, inv_re * resid_im + inv_im * resid_re])


def coefficients(medium, shift_re, shift_im):
    diag_re = 6.0 + shift_re * medium
    diag_im = shift_im * medium
    denom = diag_re * diag_re + diag_im * diag_im
    return (diag_re, diag_im, OMEGA_RELAX * diag_re / denom, -OMEGA_RELAX * diag_im / denom)


def conjugate(factors):
    return (factors[0], -factors[1], factors[2], -factors[3])


def relax_all(source, factors):
    iterate = jnp.zeros(source.shape, jnp.float32)
    for repeat in range(STEPS):
        extended = jnp.pad(iterate, ((0, 0), (0, 0), (1, 1), (0, 0), (0, 0)))
        iterate = sweep_once(extended, factors, source)
    return iterate


def reference(probes, background, medium, shifts, receivers):
    listen = receivers.astype(jnp.float32)
    total = jnp.zeros(probes.shape, jnp.float32)
    for freq_index in range(FREQS):
        shift_re = shifts[freq_index, 0]
        shift_im = shifts[freq_index, 1]
        back_re = background[freq_index, 0]
        back_im = background[freq_index, 1]
        scaled_re = shift_re * back_re - shift_im * back_im
        scaled_im = shift_re * back_im + shift_im * back_re
        source = jnp.stack([scaled_re * probes, scaled_im * probes])
        factors = coefficients(medium, shift_re, shift_im)
        forward = relax_all(source, factors)
        adjoint_field = relax_all(listen * forward, conjugate(factors))
        total = total + scaled_re * adjoint_field[0] + scaled_im * adjoint_field[1]
    return total
```

```python
import functools

import jax
import jax.numpy as jnp
from jax import lax
from jax.experimental import pallas as pl
from jax.experimental.pallas import tpu as pltpu
from jax.sharding import PartitionSpec as P

STEPS = 4
OMEGA_RELAX = 0.8
MESH = pl.DeviceIdType.MESH

PAIRS = 2
MARGIN = 8


def spread(values):
    rows, lanes = values.shape
    row = lax.broadcasted_iota(jnp.int32, values.shape, 0)
    lane = lax.broadcasted_iota(jnp.int32, values.shape, 1)
    zero = jnp.zeros_like(values)
    up = jnp.where(row == 0, zero, pltpu.roll(values, 1, 0))
    down = jnp.where(row == rows - 1, zero, pltpu.roll(values, rows - 1, 0))
    left = jnp.where(lane == 0, zero, pltpu.roll(values, 1, 1))
    right = jnp.where(lane == lanes - 1, zero, pltpu.roll(values, lanes - 1, 1))
    return (up + down) + (left + right)


def kernel(
    freqs, spaces, rows_all, shifts_ref, probes_ref, back_ref, medium_ref, receivers_ref, out_ref,
    probes_in, back_in, medium_in, listen_in, shift_out, shift_in,
    inverse, fields, halos, terms,
    send_in, recv_probes, recv_medium, recv_listen, recv_back, send_back,
    send_shift, recv_shift, send_halo, recv_halo, send_out, recv_out,
):
    own = probes_ref.shape[1]
    layers = PAIRS * own
    num_probes = probes_ref.shape[0]
    window = probes_in.shape[2]
    part = window - 2 * MARGIN
    h = lax.axis_index("freq")
    s = lax.axis_index("space")
    group = s // (2 * PAIRS)
    base = group * (2 * PAIRS)
    q = (s // 2) % PAIRS
    c = s % 2
    has_low = jnp.logical_or(c != 0, group != 0)
    has_high = jnp.logical_or(c != 1, group != spaces // (2 * PAIRS) - 1)
    low = jnp.where(c == 0, s - 3, s - 1)
    high = jnp.where(c == 0, s + 1, s + 3)

    barrier = pltpu.get_barrier_semaphore()
    for f in range(freqs):
        for member in range(2 * PAIRS):
            @pl.when(jnp.logical_not(jnp.logical_and(h == f, base + member == s)))
            def _():
                pl.semaphore_signal(barrier, inc=1, device_id=(f, base + member), device_id_type=MESH)

    @pl.when(jnp.logical_and(has_low, c == 0))
    def _():
        pl.semaphore_signal(barrier, inc=1, device_id=(h, low), device_id_type=MESH)

    @pl.when(jnp.logical_and(has_high, c == 1))
    def _():
        pl.semaphore_signal(barrier, inc=1, device_id=(h, high), device_id_type=MESH)

    pick = lax.broadcasted_iota(jnp.int32, shift_out.shape, 0)
    shift_out[...] = jnp.where(pick == 0, shifts_ref[0, 0], shifts_ref[0, 1])

    @pl.when(jnp.logical_not(has_low))
    def _():
        halos[:, 0] = jnp.zeros_like(halos[:, 0])

    @pl.when(jnp.logical_not(has_high))
    def _():
        halos[:, 1] = jnp.zeros_like(halos[:, 1])

    outside = jnp.logical_or(
        jnp.logical_and(has_low, c == 0), jnp.logical_and(has_high, c == 1)
    )
    pl.semaphore_wait(barrier, 2 * PAIRS * freqs - 1 + outside.astype(jnp.int32))

    def first_row(f, pair):
        start = jnp.clip((f * PAIRS + pair) * part - MARGIN, 0, rows_all - window)
        return pl.multiple_of(start, 8)

    def put(src, dst, send_sem, recv_sem, f, to, go):
        here = jnp.logical_and(h == f, s == to)

        @pl.when(jnp.logical_not(here))
        def _():
            copy = pltpu.make_async_remote_copy(
                src_ref=src, dst_ref=dst, send_sem=send_sem, recv_sem=recv_sem,
                device_id=(f, to), device_id_type=MESH,
            )
            if go:
                copy.start()
            else:
                copy.wait_send()

        if go:
            @pl.when(here)
            def _():
                pltpu.make_async_copy(src, dst, recv_sem).start()

    def arrived(dst, sem):
        pltpu.make_async_copy(dst, dst, sem).wait()

    mine = pl.ds(c * own, own)

    def send_inputs(go):
        for f in range(freqs):
            @pl.when(h != f)
            def _():
                copy = pltpu.make_async_remote_copy(
                    src_ref=shift_out, dst_ref=shift_in.at[h], send_sem=send_shift.at[f],
                    recv_sem=recv_shift.at[h], device_id=(f, s), device_id_type=MESH,
                )
                if go:
                    copy.start()
                else:
                    copy.wait_send()

        for pair in range(PAIRS):
            to = base + 2 * pair + q
            rows = pl.ds(first_row(h, pair), window)
            put(medium_ref.at[:, rows], medium_in.at[mine],
                send_in.at[0, pair], recv_medium.at[c], h, to, go)
            put(probes_ref.at[:, :, rows], probes_in.at[:, mine],
                send_in.at[1, pair], recv_probes.at[c], h, to, go)
        for f in range(freqs):
            for pair in range(PAIRS):
                to = base + 2 * pair + q
                rows = pl.ds(first_row(f, pair), window)
                put(back_ref.at[0, :, :, rows], back_in.at[h, :, mine],
                    send_back.at[f, pair], recv_back.at[h, c], f, to, go)
        for pair in range(PAIRS):
            to = base + 2 * pair + q
            rows = pl.ds(first_row(h, pair), window)
            put(receivers_ref.at[:, rows], listen_in.at[mine],
                send_in.at[2, pair], recv_listen.at[c], h, to, go)

    send_inputs(True)

    shift_in[h] = shift_out[...]

    def halo(k, block, side, go):
        there = has_low if side == 0 else has_high
        layer = 0 if side == 0 else layers - 1

        @pl.when(there)
        def _():
            copy = pltpu.make_async_remote_copy(
                src_ref=fields.at[k, layer, block],
                dst_ref=halos.at[k, 1 - side, block],
                send_sem=send_halo.at[k, side, block],
                recv_sem=recv_halo.at[k, 1 - side, block],
                device_id=(h, low if side == 0 else high), device_id_type=MESH,
            )
            if go:
                copy.start()
            else:
                copy.wait_send()

    def halo_arrived(k, block, side):
        there = has_low if side == 0 else has_high

        @pl.when(there)
        def _():
            arrived(halos.at[k, side, block], recv_halo.at[k, side, block])

    def scaled(f, layer):
        shift_re, shift_im = shift_in[f, 0:1], shift_in[f, 1:2]
        back_re, back_im = back_in[f, 0, layer], back_in[f, 1, layer]
        return shift_re * back_re - shift_im * back_im, shift_re * back_im + shift_im * back_re

    edges = (0, layers - 1)
    inner = tuple(range(1, layers - 1))

    for owner in range(2):
        arrived(medium_in.at[pl.ds(owner * own, own)], recv_medium.at[owner])
        arrived(probes_in.at[:, pl.ds(owner * own, own)], recv_probes.at[owner])

    def first(f, layer):
        shift_re, shift_im = shift_in[f, 0:1], shift_in[f, 1:2]
        medium = medium_in[layer]
        diag_re = 6.0 + shift_re * medium
        diag_im = shift_im * medium
        scale = OMEGA_RELAX / (diag_re * diag_re + diag_im * diag_im)
        inv_re = diag_re * scale
        inv_im = -diag_im * scale
        inverse[f, 0, layer] = inv_re
        inverse[f, 1, layer] = inv_im
        scaled_re, scaled_im = scaled(f, layer)
        start_re = inv_re * scaled_re - inv_im * scaled_im
        start_im = inv_re * scaled_im + inv_im * scaled_re
        for p in range(num_probes):
            probe = probes_in[p, layer]
            fields[0, layer, f * num_probes + p, 0] = start_re * probe
            fields[0, layer, f * num_probes + p, 1] = start_im * probe

    @pl.loop(0, freqs)
    def _(turn):
        f = lax.rem(h + turn, freqs)

        @pl.when(turn != 0)
        def _():
            arrived(shift_in.at[f], recv_shift.at[f])

        for owner in range(2):
            arrived(back_in.at[f, :, pl.ds(owner * own, own)], recv_back.at[f, owner])
        for side, layer in enumerate(edges):
            first(f, layer)
            for p in range(num_probes):
                halo(0, f * num_probes + p, side, True)
        for layer in inner:
            first(f, layer)

    def update(k, f, block, layer, sign):
        new = []
        for part_of in range(2):
            below = halos[k, 0, block, part_of] if layer == 0 else fields[k, layer - 1, block, part_of]
            above = halos[k, 1, block, part_of] if layer == layers - 1 else fields[k, layer + 1, block, part_of]
            new.append((below + above) + spread(fields[k, layer, block, part_of]))
        sum_re, sum_im = new
        inv_re = inverse[f, 0, layer]
        inv_im = sign * inverse[f, 1, layer]
        origin = 0 if k < STEPS - 1 else STEPS - 1
        keep = 1.0 - OMEGA_RELAX
        next_re = keep * fields[k, layer, block, 0] + fields[origin, layer, block, 0]
        next_im = keep * fields[k, layer, block, 1] + fields[origin, layer, block, 1]
        next_re = next_re + (inv_re * sum_re - inv_im * sum_im)
        next_im = next_im + (inv_re * sum_im + inv_im * sum_re)
        return next_re, next_im

    last = 2 * (STEPS - 1) - 1
    for k in range(last + 1):
        if k == STEPS - 2:
            for owner in range(2):
                arrived(listen_in.at[pl.ds(owner * own, own)], recv_listen.at[owner])
        sign = 1.0 if k < STEPS - 1 else -1.0

        def advance(f, block, layer, k=k, sign=sign):
            next_re, next_im = update(k, f, block, layer, sign)
            if k == STEPS - 2:
                listen = listen_in[layer].astype(jnp.float32)
                next_re = next_re * listen
                next_im = next_im * listen
                inv_re, inv_im = inverse[f, 0, layer], inverse[f, 1, layer]
                next_re, next_im = (
                    inv_re * next_re + inv_im * next_im,
                    inv_re * next_im - inv_im * next_re,
                )
            fields[k + 1, layer, block, 0] = next_re
            fields[k + 1, layer, block, 1] = next_im

        if k < last:
            @pl.loop(0, freqs)
            def _(turn):
                f = lax.rem(h + turn, freqs)
                for p in range(num_probes):
                    block = f * num_probes + p
                    for side, layer in enumerate(edges):
                        halo_arrived(k, block, side)
                        advance(f, block, layer)
                        halo(k + 1, block, side, True)

            @pl.loop(0, freqs)
            def _(f):
                for p in range(num_probes):
                    for layer in inner:
                        advance(f, f * num_probes + p, layer)

    def add_terms(f, layers_of, start):
        for layer in layers_of:
            scaled_re, scaled_im = scaled(f, layer)
            for p in range(num_probes):
                next_re, next_im = update(last, f, f * num_probes + p, layer, -1.0)
                term = scaled_re * next_re + scaled_im * next_im
                terms[p, layer] = term if start else terms[p, layer] + term

    add_terms(0, inner, True)

    @pl.loop(1, freqs)
    def _(f):
        add_terms(f, inner, False)

    for block in range(num_probes):
        halo_arrived(last, block, 0)
        halo_arrived(last, block, 1)
    add_terms(0, edges, True)

    @pl.loop(1, freqs)
    def _(f):
        for p in range(num_probes):
            halo_arrived(last, f * num_probes + p, 0)
            halo_arrived(last, f * num_probes + p, 1)
        add_terms(f, edges, False)

    inside = pl.multiple_of((h * PAIRS + q) * part - first_row(h, q), 8)

    def send_terms(go):
        for owner in range(2):
            put(terms.at[:, pl.ds(owner * own, own), pl.ds(inside, part)],
                out_ref.at[:, :, pl.ds(pl.multiple_of(q * part, 8), part)],
                send_out.at[owner], recv_out.at[q], h, base + 2 * c + owner, go)

    send_terms(True)
    for pair in range(PAIRS):
        arrived(out_ref.at[:, :, pl.ds(pair * part, part)], recv_out.at[pair])
    send_terms(False)
    send_inputs(False)

    @pl.loop(0, last + 1)
    def _(k):
        @pl.loop(0, freqs * num_probes)
        def _(block):
            halo(k, block, 0, False)
            halo(k, block, 1, False)


def per_device(freqs, spaces, probes, background, medium, shifts, receivers):
    num_probes, own, rows_all, lanes = probes.shape
    layers = PAIRS * own
    part = rows_all // (freqs * PAIRS)
    window = part + 2 * MARGIN
    blocks = freqs * num_probes
    count = 2 * (STEPS - 1)
    dma = pltpu.SemaphoreType.DMA
    any_spec = pl.BlockSpec(memory_space=pl.ANY)
    return pl.pallas_call(
        functools.partial(kernel, freqs, spaces, rows_all),
        out_shape=jax.ShapeDtypeStruct((num_probes, own, rows_all // freqs, lanes), jnp.float32),
        in_specs=[pl.BlockSpec(memory_space=pltpu.SMEM)] + [any_spec] * 4,
        out_specs=any_spec,
        scratch_shapes=[
            pltpu.VMEM((num_probes, layers, window, lanes), jnp.float32),
            pltpu.VMEM((freqs, 2, layers, window, lanes), jnp.float32),
            pltpu.VMEM((layers, window, lanes), jnp.float32),
            pltpu.VMEM((layers, window, lanes), jnp.int32),
            pltpu.VMEM((8, lanes), jnp.float32),
            pltpu.VMEM((freqs, 8, lanes), jnp.float32),
            pltpu.VMEM((freqs, 2, layers, window, lanes), jnp.float32),
            pltpu.VMEM((count, layers, blocks, 2, window, lanes), jnp.float32),
            pltpu.VMEM((count, 2, blocks, 2, window, lanes), jnp.float32),
            pltpu.VMEM((num_probes, layers, window, lanes), jnp.float32),
            dma((3, PAIRS)),
            dma((2,)),
            dma((2,)),
            dma((2,)),
            dma((freqs, 2)),
            dma((freqs, PAIRS)),
            dma((freqs,)),
            dma((freqs,)),
            dma((count, 2, blocks)),
            dma((count, 2, blocks)),
            dma((2,)),
            dma((PAIRS,)),
        ],
        compiler_params=pltpu.CompilerParams(collective_id=0, has_side_effects=True),
    )(shifts, probes, background, medium, receivers)


def solution(mesh):
    in_specs = (
        P(None, "space", None, None),
        P("freq", None, "space", None, None),
        P("space", None, None),
        P("freq", None),
        P("space", None, None),
    )
    out_specs = P(None, "space", "freq", None)
    return jax.shard_map(
        functools.partial(per_device, mesh.shape["freq"], mesh.shape["space"]),
        mesh=mesh, in_specs=in_specs, out_specs=out_specs, check_vma=False,
    )
```

```python
import functools

import jax
import jax.numpy as jnp
from jax import lax
from jax.experimental import pallas as pl
from jax.experimental.pallas import tpu as pltpu
from jax.sharding import PartitionSpec as P

STEPS = 4
OMEGA_RELAX = 0.8
MESH = pl.DeviceIdType.MESH

PAIRS = 2
MARGIN = 8
DEPTH = 2


def spread(values):
    rows, lanes = values.shape
    row = lax.broadcasted_iota(jnp.int32, values.shape, 0)
    lane = lax.broadcasted_iota(jnp.int32, values.shape, 1)
    zero = jnp.zeros_like(values)
    up = jnp.where(row == 0, zero, pltpu.roll(values, 1, 0))
    down = jnp.where(row == rows - 1, zero, pltpu.roll(values, rows - 1, 0))
    left = jnp.where(lane == 0, zero, pltpu.roll(values, 1, 1))
    right = jnp.where(lane == lanes - 1, zero, pltpu.roll(values, lanes - 1, 1))
    return (up + down) + (left + right)


def kernel(
    freqs, spaces, rows_all, shifts_ref, probes_ref, back_ref, medium_ref, receivers_ref, out_ref,
    probes_in, back_in, medium_in, listen_in, shift_out, shift_in,
    inverse, fields, terms,
    send_in, recv_probes, recv_medium, recv_listen, recv_back, send_back,
    send_shift, recv_shift, send_halo, recv_halo, send_near, recv_near, send_out, recv_out,
):
    own = probes_ref.shape[1]
    layers = PAIRS * own
    num_probes = probes_ref.shape[0]
    window = probes_in.shape[2]
    part = window - 2 * MARGIN
    last = 2 * (STEPS - 1) - 1
    sent = tuple(range(0, last, DEPTH))
    h = lax.axis_index("freq")
    s = lax.axis_index("space")
    group = s // (2 * PAIRS)
    base = group * (2 * PAIRS)
    q = (s // 2) % PAIRS
    c = s % 2
    has_low = jnp.logical_or(c != 0, group != 0)
    has_high = jnp.logical_or(c != 1, group != spaces // (2 * PAIRS) - 1)
    low = jnp.where(c == 0, s - 3, s - 1)
    high = jnp.where(c == 0, s + 1, s + 3)

    barrier = pltpu.get_barrier_semaphore()
    for f in range(freqs):
        for member in range(2 * PAIRS):
            @pl.when(jnp.logical_not(jnp.logical_and(h == f, base + member == s)))
            def _():
                pl.semaphore_signal(barrier, inc=1, device_id=(f, base + member), device_id_type=MESH)

    @pl.when(jnp.logical_and(has_low, c == 0))
    def _():
        pl.semaphore_signal(barrier, inc=1, device_id=(h, low), device_id_type=MESH)

    @pl.when(jnp.logical_and(has_high, c == 1))
    def _():
        pl.semaphore_signal(barrier, inc=1, device_id=(h, high), device_id_type=MESH)

    pick = lax.broadcasted_iota(jnp.int32, shift_out.shape, 0)
    shift_out[...] = jnp.where(pick == 0, shifts_ref[0, 0], shifts_ref[0, 1])

    @pl.when(jnp.logical_not(has_low))
    def _():
        for k in sent:
            fields[k, 0:DEPTH] = jnp.zeros_like(fields[k, 0:DEPTH])
        listen_in[0] = jnp.zeros_like(listen_in[0])

    @pl.when(jnp.logical_not(has_high))
    def _():
        for k in sent:
            fields[k, layers + DEPTH :] = jnp.zeros_like(fields[k, layers + DEPTH :])
        listen_in[layers + 1] = jnp.zeros_like(listen_in[layers + 1])

    outside = jnp.logical_or(
        jnp.logical_and(has_low, c == 0), jnp.logical_and(has_high, c == 1)
    )
    pl.semaphore_wait(barrier, 2 * PAIRS * freqs - 1 + outside.astype(jnp.int32))

    def first_row(f, pair):
        start = jnp.clip((f * PAIRS + pair) * part - MARGIN, 0, rows_all - window)
        return pl.multiple_of(start, 8)

    def put(src, dst, send_sem, recv_sem, f, to, go):
        here = jnp.logical_and(h == f, s == to)

        @pl.when(jnp.logical_not(here))
        def _():
            copy = pltpu.make_async_remote_copy(
                src_ref=src, dst_ref=dst, send_sem=send_sem, recv_sem=recv_sem,
                device_id=(f, to), device_id_type=MESH,
            )
            if go:
                copy.start()
            else:
                copy.wait_send()

        if go:
            @pl.when(here)
            def _():
                pltpu.make_async_copy(src, dst, recv_sem).start()

    def arrived(dst, sem):
        pltpu.make_async_copy(dst, dst, sem).wait()

    mine = pl.ds(c * own, own)
    mine_near = pl.ds(1 + c * own, own)

    def send_inputs(go):
        for f in range(freqs):
            @pl.when(h != f)
            def _():
                copy = pltpu.make_async_remote_copy(
                    src_ref=shift_out, dst_ref=shift_in.at[h], send_sem=send_shift.at[f],
                    recv_sem=recv_shift.at[h], device_id=(f, s), device_id_type=MESH,
                )
                if go:
                    copy.start()
                else:
                    copy.wait_send()

        def back(f):
            for step in range(PAIRS):
                pair = lax.rem(q + 1 + step, PAIRS)
                rows = pl.ds(first_row(f, pair), window)
                put(back_ref.at[0, :, :, rows], back_in.at[h, :, mine],
                    send_back.at[f, pair], recv_back.at[h, c], f, base + 2 * pair + q, go)

        def shared(index, src, dst, sem):
            for step in range(PAIRS):
                pair = lax.rem(q + 1 + step, PAIRS)
                rows = pl.ds(first_row(h, pair), window)
                put(src(rows), dst, send_in.at[index, pair], sem.at[c], h, base + 2 * pair + q, go)

        shared(0, lambda rows: medium_ref.at[:, rows], medium_in.at[mine_near], recv_medium)
        back(h)
        shared(1, lambda rows: probes_ref.at[:, :, rows], probes_in.at[:, mine], recv_probes)
        for turn in range(1, freqs):
            back(lax.rem(h + turn, freqs))
        shared(2, lambda rows: receivers_ref.at[:, rows], listen_in.at[mine_near], recv_listen)

    send_inputs(True)

    shift_in[h] = shift_out[...]

    def send(src, dst, send_sem, recv_sem, side, go):
        @pl.when(has_low if side == 0 else has_high)
        def _():
            copy = pltpu.make_async_remote_copy(
                src_ref=src, dst_ref=dst, send_sem=send_sem, recv_sem=recv_sem,
                device_id=(h, low if side == 0 else high), device_id_type=MESH,
            )
            if go:
                copy.start()
            else:
                copy.wait_send()

    def halo(k, block, side, go):
        src = pl.ds(DEPTH if side == 0 else layers, DEPTH)
        dst = pl.ds(layers + DEPTH if side == 0 else 0, DEPTH)
        send(fields.at[k, src, block], fields.at[k, dst, block],
             send_halo.at[k // DEPTH, side, block], recv_halo.at[k // DEPTH, 1 - side, block], side, go)

    def halo_arrived(k, block):
        for side in range(2):
            @pl.when(has_low if side == 0 else has_high)
            def _():
                where = pl.ds(0 if side == 0 else layers + DEPTH, DEPTH)
                arrived(fields.at[k, where, block], recv_halo.at[k // DEPTH, side, block])

    def near(ref, index, side, go):
        send(ref.at[1 if side == 0 else layers], ref.at[layers + 1 if side == 0 else 0],
             send_near.at[index, side], recv_near.at[index, 1 - side], side, go)

    def near_arrived(ref, index):
        for side in range(2):
            @pl.when(has_low if side == 0 else has_high)
            def _():
                arrived(ref.at[0 if side == 0 else layers + 1], recv_near.at[index, side])

    def scaled(f, layer):
        shift_re, shift_im = shift_in[f, 0:1], shift_in[f, 1:2]
        back_re, back_im = back_in[f, 0, layer], back_in[f, 1, layer]
        return shift_re * back_re - shift_im * back_im, shift_re * back_im + shift_im * back_re

    def invert(f, index):
        shift_re, shift_im = shift_in[f, 0:1], shift_in[f, 1:2]
        medium = medium_in[index]
        diag_re = 6.0 + shift_re * medium
        diag_im = shift_im * medium
        scale = OMEGA_RELAX / (diag_re * diag_re + diag_im * diag_im)
        inv_re = diag_re * scale
        inv_im = -diag_im * scale
        inverse[f, 0, index] = inv_re
        inverse[f, 1, index] = inv_im
        return inv_re, inv_im

    order = list(range(DEPTH)) + [i for i in range(layers - DEPTH, layers) if i >= DEPTH]
    order += [i for i in range(layers) if i not in order]
    ready_low, ready_high = DEPTH, min(2 * DEPTH, layers)

    for owner in range(2):
        arrived(medium_in.at[pl.ds(1 + owner * own, own)], recv_medium.at[owner])
    for side in range(2):
        near(medium_in, 0, side, True)

    def first(turn):
        f = lax.rem(h + turn, freqs)

        @pl.when(turn != 0)
        def _():
            arrived(shift_in.at[f], recv_shift.at[f])

        for owner in range(2):
            arrived(back_in.at[f, :, pl.ds(owner * own, own)], recv_back.at[f, owner])

        @pl.when(turn == 0)
        def _():
            for owner in range(2):
                arrived(probes_in.at[:, pl.ds(owner * own, own)], recv_probes.at[owner])

        for done, layer in enumerate(order):
            inv_re, inv_im = invert(f, 1 + layer)
            scaled_re, scaled_im = scaled(f, layer)
            start_re = inv_re * scaled_re - inv_im * scaled_im
            start_im = inv_re * scaled_im + inv_im * scaled_re
            for p in range(num_probes):
                block = f * num_probes + p
                probe = probes_in[p, layer]
                fields[0, DEPTH + layer, block, 0] = start_re * probe
                fields[0, DEPTH + layer, block, 1] = start_im * probe
                if done + 1 == ready_low:
                    halo(0, block, 0, True)
                if done + 1 == ready_high:
                    halo(0, block, 1, True)

    pl.loop(0, freqs)(first)

    def update(k, f, block, at, sign):
        new = []
        for part_of in range(2):
            beside = fields[k, at - 1, block, part_of] + fields[k, at + 1, block, part_of]
            new.append(beside + spread(fields[k, at, block, part_of]))
        sum_re, sum_im = new
        inv_re = inverse[f, 0, at - 1]
        inv_im = sign * inverse[f, 1, at - 1]
        origin = 0 if k < STEPS - 1 else STEPS - 1
        keep = 1.0 - OMEGA_RELAX
        next_re = keep * fields[k, at, block, 0] + fields[origin, at, block, 0]
        next_im = keep * fields[k, at, block, 1] + fields[origin, at, block, 1]
        next_re = next_re + (inv_re * sum_re - inv_im * sum_im)
        next_im = next_im + (inv_re * sum_im + inv_im * sum_re)
        return next_re, next_im

    def advance(k, f, block, at):
        next_re, next_im = update(k, f, block, at, 1.0 if k < STEPS - 1 else -1.0)
        if k == STEPS - 2:
            listen = listen_in[at - 1].astype(jnp.float32)
            next_re = next_re * listen
            next_im = next_im * listen
            inv_re, inv_im = inverse[f, 0, at - 1], inverse[f, 1, at - 1]
            next_re, next_im = (
                inv_re * next_re + inv_im * next_im,
                inv_re * next_im - inv_im * next_re,
            )
        fields[k + 1, at, block, 0] = next_re
        fields[k + 1, at, block, 1] = next_im

    def invert_near(f):
        for side in range(2):
            there = has_low if side == 0 else has_high
            index = 0 if side == 0 else layers + 1

            @pl.when(there)
            def _():
                invert(f, index)

            @pl.when(jnp.logical_not(there))
            def _():
                inverse[f, :, index] = jnp.zeros_like(inverse[f, :, index])

    for k in sent[:-1]:
        if k == 0:
            near_arrived(medium_in, 0)
        if k == DEPTH:
            near_arrived(listen_in, 1)

        @pl.loop(0, freqs)
        def _(turn, k=k):
            f = lax.rem(h + turn, freqs)
            if k == 0:
                invert_near(f)
            for p in range(num_probes):
                block = f * num_probes + p
                halo_arrived(k, block)
                for at in range(1, layers + 3):
                    advance(k, f, block, at)
                for done, layer in enumerate(order):
                    advance(k + 1, f, block, DEPTH + layer)
                    if done + 1 == ready_low:
                        halo(k + DEPTH, block, 0, True)
                    if done + 1 == ready_high:
                        halo(k + DEPTH, block, 1, True)

        if k == 0:
            for owner in range(2):
                arrived(listen_in.at[pl.ds(1 + owner * own, own)], recv_listen.at[owner])
            for side in range(2):
                near(listen_in, 1, side, True)

    inside = pl.multiple_of((h * PAIRS + q) * part - first_row(h, q), 8)

    def send_terms(p, go):
        for owner in range(2):
            put(terms.at[p, pl.ds(owner * own, own), pl.ds(inside, part)],
                out_ref.at[p, :, pl.ds(pl.multiple_of(q * part, 8), part)],
                send_out.at[p, owner], recv_out.at[p, q], h, base + 2 * c + owner, go)

    def add_terms(f, p, start):
        block = f * num_probes + p
        halo_arrived(last - 1, block)
        for at in range(1, layers + 3):
            advance(last - 1, f, block, at)
        for layer in range(layers):
            scaled_re, scaled_im = scaled(f, layer)
            next_re, next_im = update(last, f, block, DEPTH + layer, -1.0)
            term = scaled_re * next_re + scaled_im * next_im
            terms[p, layer] = term if start else terms[p, layer] + term

    for p in range(num_probes):
        add_terms(h, p, True)

    if freqs > 2:
        @pl.loop(1, freqs - 1)
        def _(turn):
            for p in range(num_probes):
                add_terms(lax.rem(h + turn, freqs), p, False)

    for p in range(num_probes):
        if freqs > 1:
            add_terms(lax.rem(h + freqs - 1, freqs), p, False)
        send_terms(p, True)

    for p in range(num_probes):
        for pair in range(PAIRS):
            arrived(out_ref.at[p, :, pl.ds(pair * part, part)], recv_out.at[p, pair])
    for p in range(num_probes):
        send_terms(p, False)
    send_inputs(False)
    for side in range(2):
        near(medium_in, 0, side, False)
        near(listen_in, 1, side, False)
    for k in sent:
        @pl.loop(0, freqs * num_probes)
        def _(block, k=k):
            halo(k, block, 0, False)
            halo(k, block, 1, False)


def per_device(freqs, spaces, probes, background, medium, shifts, receivers):
    num_probes, own, rows_all, lanes = probes.shape
    layers = PAIRS * own
    part = rows_all // (freqs * PAIRS)
    window = part + 2 * MARGIN
    blocks = freqs * num_probes
    count = 2 * (STEPS - 1)
    dma = pltpu.SemaphoreType.DMA
    any_spec = pl.BlockSpec(memory_space=pl.ANY)
    return pl.pallas_call(
        functools.partial(kernel, freqs, spaces, rows_all),
        out_shape=jax.ShapeDtypeStruct((num_probes, own, rows_all // freqs, lanes), jnp.float32),
        in_specs=[pl.BlockSpec(memory_space=pltpu.SMEM)] + [any_spec] * 4,
        out_specs=any_spec,
        scratch_shapes=[
            pltpu.VMEM((num_probes, layers, window, lanes), jnp.float32),
            pltpu.VMEM((freqs, 2, layers, window, lanes), jnp.float32),
            pltpu.VMEM((layers + 2, window, lanes), jnp.float32),
            pltpu.VMEM((layers + 2, window, lanes), jnp.int32),
            pltpu.VMEM((8, lanes), jnp.float32),
            pltpu.VMEM((freqs, 8, lanes), jnp.float32),
            pltpu.VMEM((freqs, 2, layers + 2, window, lanes), jnp.float32),
            pltpu.VMEM((count, layers + 2 * DEPTH, blocks, 2, window, lanes), jnp.float32),
            pltpu.VMEM((num_probes, layers, window, lanes), jnp.float32),
            dma((3, PAIRS)),
            dma((2,)),
            dma((2,)),
            dma((2,)),
            dma((freqs, 2)),
            dma((freqs, PAIRS)),
            dma((freqs,)),
            dma((freqs,)),
            dma((count // DEPTH, 2, blocks)),
            dma((count // DEPTH, 2, blocks)),
            dma((2, 2)),
            dma((2, 2)),
            dma((num_probes, 2)),
            dma((num_probes, PAIRS)),
        ],
        compiler_params=pltpu.CompilerParams(collective_id=0, has_side_effects=True),
    )(shifts, probes, background, medium, receivers)


def solution(mesh):
    in_specs = (
        P(None, "space", None, None),
        P("freq", None, "space", None, None),
        P("space", None, None),
        P("freq", None),
        P("space", None, None),
    )
    out_specs = P(None, "space", "freq", None)
    return jax.shard_map(
        functools.partial(per_device, mesh.shape["freq"], mesh.shape["space"]),
        mesh=mesh, in_specs=in_specs, out_specs=out_specs, check_vma=False,
    )
```

```python
import functools

import jax
import jax.numpy as jnp
from jax import lax
from jax.experimental import pallas as pl
from jax.experimental.pallas import tpu as pltpu
from jax.sharding import PartitionSpec as P

STEPS = 4
OMEGA_RELAX = 0.8
MESH = pl.DeviceIdType.MESH

PAIRS = 2
MARGIN = 8
DEPTH = 2


def spread(values):
    rows, lanes = values.shape
    row = lax.broadcasted_iota(jnp.int32, values.shape, 0)
    lane = lax.broadcasted_iota(jnp.int32, values.shape, 1)
    zero = jnp.zeros_like(values)
    up = jnp.where(row == 0, zero, pltpu.roll(values, 1, 0))
    down = jnp.where(row == rows - 1, zero, pltpu.roll(values, rows - 1, 0))
    left = jnp.where(lane == 0, zero, pltpu.roll(values, 1, 1))
    right = jnp.where(lane == lanes - 1, zero, pltpu.roll(values, lanes - 1, 1))
    return (up + down) + (left + right)


def kernel(
    freqs, spaces, rows_all, shifts_ref, probes_ref, back_ref, medium_ref, receivers_ref, out_ref,
    probes_in, back_in, medium_in, listen_in, shift_out, shift_in,
    inverse, start, fields, terms,
    send_in, recv_probes, recv_medium, recv_listen, recv_back, send_back,
    send_shift, recv_shift, send_halo, recv_halo, send_far, recv_far, send_near, recv_near, send_out, recv_out,
):
    own = probes_ref.shape[1]
    layers = PAIRS * own
    num_probes = probes_ref.shape[0]
    window = probes_in.shape[2]
    part = window - 2 * MARGIN
    last = 2 * (STEPS - 1) - 1
    sent = tuple(range(0, last, DEPTH))
    h = lax.axis_index("freq")
    s = lax.axis_index("space")
    group = s // (2 * PAIRS)
    base = group * (2 * PAIRS)
    q = (s // 2) % PAIRS
    c = s % 2
    has_low = jnp.logical_or(c != 0, group != 0)
    has_high = jnp.logical_or(c != 1, group != spaces // (2 * PAIRS) - 1)
    low = jnp.where(c == 0, s - 3, s - 1)
    high = jnp.where(c == 0, s + 1, s + 3)

    barrier = pltpu.get_barrier_semaphore()
    for f in range(freqs):
        for member in range(2 * PAIRS):
            @pl.when(jnp.logical_not(jnp.logical_and(h == f, base + member == s)))
            def _():
                pl.semaphore_signal(barrier, inc=1, device_id=(f, base + member), device_id_type=MESH)

    @pl.when(jnp.logical_and(has_low, c == 0))
    def _():
        pl.semaphore_signal(barrier, inc=1, device_id=(h, low), device_id_type=MESH)

    @pl.when(jnp.logical_and(has_high, c == 1))
    def _():
        pl.semaphore_signal(barrier, inc=1, device_id=(h, high), device_id_type=MESH)

    pick = lax.broadcasted_iota(jnp.int32, shift_out.shape, 0)
    shift_out[...] = jnp.where(pick == 0, shifts_ref[0, 0], shifts_ref[0, 1])

    @pl.when(jnp.logical_not(has_low))
    def _():
        for k in sent:
            fields[k, 0:DEPTH] = jnp.zeros_like(fields[k, 0:DEPTH])
        listen_in[0] = jnp.zeros_like(listen_in[0])

    @pl.when(jnp.logical_not(has_high))
    def _():
        for k in sent:
            fields[k, layers + DEPTH :] = jnp.zeros_like(fields[k, layers + DEPTH :])
        listen_in[layers + 1] = jnp.zeros_like(listen_in[layers + 1])

    outside = jnp.logical_or(
        jnp.logical_and(has_low, c == 0), jnp.logical_and(has_high, c == 1)
    )
    pl.semaphore_wait(barrier, 2 * PAIRS * freqs - 1 + outside.astype(jnp.int32))

    def first_row(f, pair):
        start = jnp.clip((f * PAIRS + pair) * part - MARGIN, 0, rows_all - window)
        return pl.multiple_of(start, 8)

    def put(src, dst, send_sem, recv_sem, f, to, go):
        here = jnp.logical_and(h == f, s == to)

        @pl.when(jnp.logical_not(here))
        def _():
            copy = pltpu.make_async_remote_copy(
                src_ref=src, dst_ref=dst, send_sem=send_sem, recv_sem=recv_sem,
                device_id=(f, to), device_id_type=MESH,
            )
            if go:
                copy.start()
            else:
                copy.wait_send()

        if go:
            @pl.when(here)
            def _():
                pltpu.make_async_copy(src, dst, recv_sem).start()

    def arrived(dst, sem):
        pltpu.make_async_copy(dst, dst, sem).wait()

    mine = pl.ds(c * own, own)
    mine_near = pl.ds(1 + c * own, own)

    def send_inputs(go):
        for f in range(freqs):
            @pl.when(h != f)
            def _():
                copy = pltpu.make_async_remote_copy(
                    src_ref=shift_out, dst_ref=shift_in.at[h], send_sem=send_shift.at[f],
                    recv_sem=recv_shift.at[h], device_id=(f, s), device_id_type=MESH,
                )
                if go:
                    copy.start()
                else:
                    copy.wait_send()

        def back(f):
            for step in range(PAIRS):
                pair = lax.rem(q + 1 + step, PAIRS)
                rows = pl.ds(first_row(f, pair), window)
                put(back_ref.at[0, :, :, rows], back_in.at[h, :, mine],
                    send_back.at[f, pair], recv_back.at[h, c], f, base + 2 * pair + q, go)

        def shared(index, src, dst, sem):
            for step in range(PAIRS):
                pair = lax.rem(q + 1 + step, PAIRS)
                rows = pl.ds(first_row(h, pair), window)
                put(src(rows), dst, send_in.at[index, pair], sem.at[c], h, base + 2 * pair + q, go)

        shared(0, lambda rows: medium_ref.at[:, rows], medium_in.at[mine_near], recv_medium)
        back(h)
        for p in range(num_probes):
            shared(2 + p, lambda rows: probes_ref.at[p, :, rows], probes_in.at[p, mine], recv_probes.at[p])
        shared(1, lambda rows: receivers_ref.at[:, rows], listen_in.at[mine_near], recv_listen)
        for turn in range(1, freqs):
            back(lax.rem(h + turn, freqs))

    send_inputs(True)

    shift_in[h] = shift_out[...]

    def send(src, dst, send_sem, recv_sem, side, go):
        @pl.when(has_low if side == 0 else has_high)
        def _():
            copy = pltpu.make_async_remote_copy(
                src_ref=src, dst_ref=dst, send_sem=send_sem, recv_sem=recv_sem,
                device_id=(h, low if side == 0 else high), device_id_type=MESH,
            )
            if go:
                copy.start()
            else:
                copy.wait_send()

    inside = pl.ds(pl.multiple_of((h * PAIRS + q) * part - first_row(h, q), 8), part)

    def halo(k, block, side, go):
        if k == sent[-1]:
            src, dst = (DEPTH, layers + DEPTH) if side == 0 else (layers + 1, 1)
            send(fields.at[k, src, block], fields.at[k, dst, block],
                 send_halo.at[k // DEPTH, side, block], recv_halo.at[k // DEPTH, 1 - side, block], side, go)
            src, dst = (src + 1, dst + 1) if side == 0 else (src - 1, dst - 1)
            send(fields.at[k, src, block, :, inside], fields.at[k, dst, block, :, inside],
                 send_far.at[side, block], recv_far.at[1 - side, block], side, go)
            return
        src = pl.ds(DEPTH if side == 0 else layers, DEPTH)
        dst = pl.ds(layers + DEPTH if side == 0 else 0, DEPTH)
        send(fields.at[k, src, block], fields.at[k, dst, block],
             send_halo.at[k // DEPTH, side, block], recv_halo.at[k // DEPTH, 1 - side, block], side, go)

    def halo_arrived(k, block):
        for side in range(2):
            @pl.when(has_low if side == 0 else has_high)
            def _():
                if k == sent[-1]:
                    at, far = (1, 0) if side == 0 else (layers + DEPTH, layers + DEPTH + 1)
                    arrived(fields.at[k, at, block], recv_halo.at[k // DEPTH, side, block])
                    arrived(fields.at[k, far, block, :, inside], recv_far.at[side, block])
                else:
                    where = pl.ds(0 if side == 0 else layers + DEPTH, DEPTH)
                    arrived(fields.at[k, where, block], recv_halo.at[k // DEPTH, side, block])

    def near(ref, index, side, go):
        send(ref.at[1 if side == 0 else layers], ref.at[layers + 1 if side == 0 else 0],
             send_near.at[index, side], recv_near.at[index, 1 - side], side, go)

    def near_arrived(ref, index):
        for side in range(2):
            @pl.when(has_low if side == 0 else has_high)
            def _():
                arrived(ref.at[0 if side == 0 else layers + 1], recv_near.at[index, side])

    def scaled(f, layer):
        shift_re, shift_im = shift_in[f, 0:1], shift_in[f, 1:2]
        back_re, back_im = back_in[f, 0, layer], back_in[f, 1, layer]
        return shift_re * back_re - shift_im * back_im, shift_re * back_im + shift_im * back_re

    def invert(f, index):
        shift_re, shift_im = shift_in[f, 0:1], shift_in[f, 1:2]
        medium = medium_in[index]
        diag_re = 6.0 + shift_re * medium
        diag_im = shift_im * medium
        scale = OMEGA_RELAX / (diag_re * diag_re + diag_im * diag_im)
        inv_re = diag_re * scale
        inv_im = -diag_im * scale
        inverse[f, 0, index] = inv_re
        inverse[f, 1, index] = inv_im
        return inv_re, inv_im

    order = list(range(DEPTH)) + [i for i in range(layers - DEPTH, layers) if i >= DEPTH]
    order += [i for i in range(layers) if i not in order]
    ready_low, ready_high = DEPTH, min(2 * DEPTH, layers)

    for owner in range(2):
        arrived(medium_in.at[pl.ds(1 + owner * own, own)], recv_medium.at[owner])
    for side in range(2):
        near(medium_in, 0, side, True)

    def first(turn):
        f = lax.rem(h + turn, freqs)

        @pl.when(turn != 0)
        def _():
            arrived(shift_in.at[f], recv_shift.at[f])

        for owner in range(2):
            arrived(back_in.at[f, :, pl.ds(owner * own, own)], recv_back.at[f, owner])

        for p in range(num_probes):
            block = f * num_probes + p

            @pl.when(turn == 0)
            def _():
                for owner in range(2):
                    arrived(probes_in.at[p, pl.ds(owner * own, own)], recv_probes.at[p, owner])

            for done, layer in enumerate(order):
                if p == 0:
                    inv_re, inv_im = invert(f, 1 + layer)
                    scaled_re, scaled_im = scaled(f, layer)
                    start[0, layer] = inv_re * scaled_re - inv_im * scaled_im
                    start[1, layer] = inv_re * scaled_im + inv_im * scaled_re
                probe = probes_in[p, layer]
                fields[0, DEPTH + layer, block, 0] = start[0, layer] * probe
                fields[0, DEPTH + layer, block, 1] = start[1, layer] * probe
                if done + 1 == ready_low:
                    halo(0, block, 0, True)
                if done + 1 == ready_high:
                    halo(0, block, 1, True)

    first(0)
    for owner in range(2):
        arrived(listen_in.at[pl.ds(1 + owner * own, own)], recv_listen.at[owner])
    for side in range(2):
        near(listen_in, 1, side, True)
    pl.loop(1, freqs)(first)

    def update(k, f, block, at, sign):
        new = []
        for part_of in range(2):
            beside = fields[k, at - 1, block, part_of] + fields[k, at + 1, block, part_of]
            new.append(beside + spread(fields[k, at, block, part_of]))
        sum_re, sum_im = new
        inv_re = inverse[f, 0, at - 1]
        inv_im = sign * inverse[f, 1, at - 1]
        origin = 0 if k < STEPS - 1 else STEPS - 1
        keep = 1.0 - OMEGA_RELAX
        next_re = keep * fields[k, at, block, 0] + fields[origin, at, block, 0]
        next_im = keep * fields[k, at, block, 1] + fields[origin, at, block, 1]
        next_re = next_re + (inv_re * sum_re - inv_im * sum_im)
        next_im = next_im + (inv_re * sum_im + inv_im * sum_re)
        return next_re, next_im

    def advance(k, f, block, at):
        next_re, next_im = update(k, f, block, at, 1.0 if k < STEPS - 1 else -1.0)
        if k == STEPS - 2:
            listen = listen_in[at - 1].astype(jnp.float32)
            next_re = next_re * listen
            next_im = next_im * listen
            inv_re, inv_im = inverse[f, 0, at - 1], inverse[f, 1, at - 1]
            next_re, next_im = (
                inv_re * next_re + inv_im * next_im,
                inv_re * next_im - inv_im * next_re,
            )
        fields[k + 1, at, block, 0] = next_re
        fields[k + 1, at, block, 1] = next_im

    def invert_near(f):
        for side in range(2):
            there = has_low if side == 0 else has_high
            index = 0 if side == 0 else layers + 1

            @pl.when(there)
            def _():
                invert(f, index)

            @pl.when(jnp.logical_not(there))
            def _():
                inverse[f, :, index] = jnp.zeros_like(inverse[f, :, index])

    for k in sent[:-1]:
        if k == 0:
            near_arrived(medium_in, 0)
        if k == DEPTH:
            near_arrived(listen_in, 1)

        @pl.loop(0, freqs)
        def _(turn, k=k):
            f = lax.rem(h + turn, freqs)
            if k == 0:
                invert_near(f)
            for p in range(num_probes):
                block = f * num_probes + p
                halo_arrived(k, block)
                for at in range(1, layers + 3):
                    advance(k, f, block, at)
                for done, layer in enumerate(order):
                    advance(k + 1, f, block, DEPTH + layer)
                    if done + 1 == ready_low:
                        halo(k + DEPTH, block, 0, True)
                    if done + 1 == ready_high:
                        halo(k + DEPTH, block, 1, True)

    def send_terms(p, go):
        for owner in range(2):
            put(terms.at[p, pl.ds(owner * own, own), inside],
                out_ref.at[p, :, pl.ds(pl.multiple_of(q * part, 8), part)],
                send_out.at[p, owner], recv_out.at[p, q], h, base + 2 * c + owner, go)

    def add_terms(f, p, start):
        block = f * num_probes + p
        halo_arrived(last - 1, block)
        for at in range(1, layers + 3):
            advance(last - 1, f, block, at)
        for layer in range(layers):
            scaled_re, scaled_im = scaled(f, layer)
            next_re, next_im = update(last, f, block, DEPTH + layer, -1.0)
            term = scaled_re * next_re + scaled_im * next_im
            terms[p, layer] = term if start else terms[p, layer] + term

    for p in range(num_probes):
        add_terms(h, p, True)

    if freqs > 2:
        @pl.loop(1, freqs - 1)
        def _(turn):
            for p in range(num_probes):
                add_terms(lax.rem(h + turn, freqs), p, False)

    for p in range(num_probes):
        if freqs > 1:
            add_terms(lax.rem(h + freqs - 1, freqs), p, False)
        send_terms(p, True)

    for p in range(num_probes):
        for pair in range(PAIRS):
            arrived(out_ref.at[p, :, pl.ds(pair * part, part)], recv_out.at[p, pair])
    for p in range(num_probes):
        send_terms(p, False)
    send_inputs(False)
    for side in range(2):
        near(medium_in, 0, side, False)
        near(listen_in, 1, side, False)
    for k in sent:
        @pl.loop(0, freqs * num_probes)
        def _(block, k=k):
            halo(k, block, 0, False)
            halo(k, block, 1, False)


def per_device(freqs, spaces, probes, background, medium, shifts, receivers):
    num_probes, own, rows_all, lanes = probes.shape
    layers = PAIRS * own
    part = rows_all // (freqs * PAIRS)
    window = part + 2 * MARGIN
    blocks = freqs * num_probes
    count = 2 * (STEPS - 1)
    dma = pltpu.SemaphoreType.DMA
    any_spec = pl.BlockSpec(memory_space=pl.ANY)
    return pl.pallas_call(
        functools.partial(kernel, freqs, spaces, rows_all),
        out_shape=jax.ShapeDtypeStruct((num_probes, own, rows_all // freqs, lanes), jnp.float32),
        in_specs=[pl.BlockSpec(memory_space=pltpu.SMEM)] + [any_spec] * 4,
        out_specs=any_spec,
        scratch_shapes=[
            pltpu.VMEM((num_probes, layers, window, lanes), jnp.float32),
            pltpu.VMEM((freqs, 2, layers, window, lanes), jnp.float32),
            pltpu.VMEM((layers + 2, window, lanes), jnp.float32),
            pltpu.VMEM((layers + 2, window, lanes), jnp.int32),
            pltpu.VMEM((8, lanes), jnp.float32),
            pltpu.VMEM((freqs, 8, lanes), jnp.float32),
            pltpu.VMEM((freqs, 2, layers + 2, window, lanes), jnp.float32),
            pltpu.VMEM((2, layers, window, lanes), jnp.float32),
            pltpu.VMEM((count, layers + 2 * DEPTH, blocks, 2, window, lanes), jnp.float32),
            pltpu.VMEM((num_probes, layers, window, lanes), jnp.float32),
            dma((2 + num_probes, PAIRS)),
            dma((num_probes, 2)),
            dma((2,)),
            dma((2,)),
            dma((freqs, 2)),
            dma((freqs, PAIRS)),
            dma((freqs,)),
            dma((freqs,)),
            dma((count // DEPTH, 2, blocks)),
            dma((count // DEPTH, 2, blocks)),
            dma((2, blocks)),
            dma((2, blocks)),
            dma((2, 2)),
            dma((2, 2)),
            dma((num_probes, 2)),
            dma((num_probes, PAIRS)),
        ],
        compiler_params=pltpu.CompilerParams(collective_id=0, has_side_effects=True),
    )(shifts, probes, background, medium, receivers)


def solution(mesh):
    in_specs = (
        P(None, "space", None, None),
        P("freq", None, "space", None, None),
        P("space", None, None),
        P("freq", None),
        P("space", None, None),
    )
    out_specs = P(None, "space", "freq", None)
    return jax.shard_map(
        functools.partial(per_device, mesh.shape["freq"], mesh.shape["space"]),
        mesh=mesh, in_specs=in_specs, out_specs=out_specs, check_vma=False,
    )
```

```python
import functools

import jax
import jax.numpy as jnp
from jax import lax
from jax.experimental import pallas as pl
from jax.experimental.pallas import tpu as pltpu
from jax.sharding import PartitionSpec as P

STEPS = 4
OMEGA_RELAX = 0.8
MESH = pl.DeviceIdType.MESH

PAIRS = 2
MARGIN = 8
DEPTH = 2


def spread(values):
    rows, lanes = values.shape
    row = lax.broadcasted_iota(jnp.int32, values.shape, 0)
    lane = lax.broadcasted_iota(jnp.int32, values.shape, 1)
    zero = jnp.zeros_like(values)
    up = jnp.where(row == 0, zero, pltpu.roll(values, 1, 0))
    down = jnp.where(row == rows - 1, zero, pltpu.roll(values, rows - 1, 0))
    left = jnp.where(lane == 0, zero, pltpu.roll(values, 1, 1))
    right = jnp.where(lane == lanes - 1, zero, pltpu.roll(values, lanes - 1, 1))
    return (up + down) + (left + right)


def kernel(
    freqs, spaces, rows_all, shifts_ref, probes_ref, back_ref, medium_ref, receivers_ref, out_ref,
    probes_in, back_in, medium_in, listen_in, shift_out, shift_in,
    inverse, start, margin_out, margin_in, fields, terms,
    send_in, recv_probes, recv_medium, recv_listen, recv_back, send_back,
    send_shift, recv_shift, send_halo, recv_halo, send_far, recv_far, send_near, recv_near, send_out, recv_out,
):
    own = probes_ref.shape[1]
    layers = PAIRS * own
    num_probes = probes_ref.shape[0]
    window = probes_in.shape[2]
    part = window - 2 * MARGIN
    last = 2 * (STEPS - 1) - 1
    sent = tuple(range(0, last, DEPTH))
    h = lax.axis_index("freq")
    s = lax.axis_index("space")
    group = s // (2 * PAIRS)
    base = group * (2 * PAIRS)
    q = (s // 2) % PAIRS
    c = s % 2
    has_low = jnp.logical_or(c != 0, group != 0)
    has_high = jnp.logical_or(c != 1, group != spaces // (2 * PAIRS) - 1)
    low = jnp.where(c == 0, s - 3, s - 1)
    high = jnp.where(c == 0, s + 1, s + 3)

    barrier = pltpu.get_barrier_semaphore()
    for f in range(freqs):
        for member in range(2 * PAIRS):
            @pl.when(jnp.logical_not(jnp.logical_and(h == f, base + member == s)))
            def _():
                pl.semaphore_signal(barrier, inc=1, device_id=(f, base + member), device_id_type=MESH)

    @pl.when(jnp.logical_and(has_low, c == 0))
    def _():
        pl.semaphore_signal(barrier, inc=1, device_id=(h, low), device_id_type=MESH)

    @pl.when(jnp.logical_and(has_high, c == 1))
    def _():
        pl.semaphore_signal(barrier, inc=1, device_id=(h, high), device_id_type=MESH)

    pick = lax.broadcasted_iota(jnp.int32, shift_out.shape, 0)
    shift_out[...] = jnp.where(pick == 0, shifts_ref[0, 0], shifts_ref[0, 1])

    @pl.when(jnp.logical_not(has_low))
    def _():
        for k in sent:
            fields[k, 0:DEPTH] = jnp.zeros_like(fields[k, 0:DEPTH])
        listen_in[0] = jnp.zeros_like(listen_in[0])

    @pl.when(jnp.logical_not(has_high))
    def _():
        for k in sent:
            fields[k, layers + DEPTH :] = jnp.zeros_like(fields[k, layers + DEPTH :])
        listen_in[layers + 1] = jnp.zeros_like(listen_in[layers + 1])

    outside = jnp.logical_or(
        jnp.logical_and(has_low, c == 0), jnp.logical_and(has_high, c == 1)
    )
    pl.semaphore_wait(barrier, 2 * PAIRS * freqs - 1 + outside.astype(jnp.int32))

    def first_row(f, pair):
        start = jnp.clip((f * PAIRS + pair) * part - MARGIN, 0, rows_all - window)
        return pl.multiple_of(start, 8)

    def put(src, dst, send_sem, recv_sem, f, to, go):
        here = jnp.logical_and(h == f, s == to)

        @pl.when(jnp.logical_not(here))
        def _():
            copy = pltpu.make_async_remote_copy(
                src_ref=src, dst_ref=dst, send_sem=send_sem, recv_sem=recv_sem,
                device_id=(f, to), device_id_type=MESH,
            )
            if go:
                copy.start()
            else:
                copy.wait_send()

        if go:
            @pl.when(here)
            def _():
                pltpu.make_async_copy(src, dst, recv_sem).start()

    def arrived(dst, sem):
        pltpu.make_async_copy(dst, dst, sem).wait()

    mine = pl.ds(c * own, own)
    mine_near = pl.ds(1 + c * own, own)

    def send_inputs(go):
        for f in range(freqs):
            @pl.when(h != f)
            def _():
                copy = pltpu.make_async_remote_copy(
                    src_ref=shift_out, dst_ref=shift_in.at[h], send_sem=send_shift.at[f],
                    recv_sem=recv_shift.at[h], device_id=(f, s), device_id_type=MESH,
                )
                if go:
                    copy.start()
                else:
                    copy.wait_send()

        def back(f):
            for step in range(PAIRS):
                pair = lax.rem(q + 1 + step, PAIRS)
                rows = pl.ds(first_row(f, pair), window)
                put(back_ref.at[0, :, :, rows], back_in.at[h, :, mine],
                    send_back.at[f, pair], recv_back.at[h, c], f, base + 2 * pair + q, go)

        def shared(index, src, dst, sem):
            for step in range(PAIRS):
                pair = lax.rem(q + 1 + step, PAIRS)
                rows = pl.ds(first_row(h, pair), window)
                put(src(rows), dst, send_in.at[index, pair], sem.at[c], h, base + 2 * pair + q, go)

        shared(0, lambda rows: medium_ref.at[:, rows], medium_in.at[mine_near], recv_medium)
        back(h)
        for p in range(num_probes):
            shared(2 + p, lambda rows: probes_ref.at[p, :, rows], probes_in.at[p, mine], recv_probes.at[p])
        shared(1, lambda rows: receivers_ref.at[:, rows], listen_in.at[mine_near], recv_listen)
        for turn in range(1, freqs):
            back(lax.rem(h + turn, freqs))

    send_inputs(True)

    shift_in[h] = shift_out[...]

    def send(src, dst, send_sem, recv_sem, side, go):
        @pl.when(has_low if side == 0 else has_high)
        def _():
            copy = pltpu.make_async_remote_copy(
                src_ref=src, dst_ref=dst, send_sem=send_sem, recv_sem=recv_sem,
                device_id=(h, low if side == 0 else high), device_id_type=MESH,
            )
            if go:
                copy.start()
            else:
                copy.wait_send()

    inside_at = pl.multiple_of((h * PAIRS + q) * part - first_row(h, q), 8)
    inside = pl.ds(inside_at, part)
    tile_low = pl.ds(pl.multiple_of(jnp.maximum(inside_at - 8, 0), 8), 8)
    tile_high = pl.ds(pl.multiple_of(jnp.minimum(inside_at + part, window - 8), 8), 8)

    def margin_items(k, side, src_side):
        if k == sent[-1]:
            if src_side:
                return ((2, DEPTH if side == 0 else layers + 1),)
            return ((2, 1 if side == 0 else layers + DEPTH),)
        first_layer = (DEPTH if side == 0 else layers) if src_side else (0 if side == 0 else layers + DEPTH)
        return tuple((item, first_layer + item) for item in range(DEPTH))

    def halo(k, block, side, go):
        src = pl.ds(DEPTH if side == 0 else layers, DEPTH)
        dst = pl.ds(layers + DEPTH if side == 0 else 0, DEPTH)
        if k == 0:
            send(fields.at[k, src, block], fields.at[k, dst, block],
                 send_halo.at[k // DEPTH, side, block], recv_halo.at[k // DEPTH, 1 - side, block], side, go)
            return
        items = margin_items(k, side, True)
        if go:
            for item, at in items:
                for part_of in range(2):
                    low_rows = fields[k, at, block, part_of, tile_low]
                    high_rows = fields[k, at, block, part_of, tile_high]
                    row = lax.broadcasted_iota(jnp.int32, low_rows.shape, 0)
                    margin_out[side, block, item, part_of] = jnp.where(row < 4, high_rows, low_rows)
        send(fields.at[k, src, block, :, inside], fields.at[k, dst, block, :, inside],
             send_halo.at[k // DEPTH, side, block], recv_halo.at[k // DEPTH, 1 - side, block], side, go)
        which = pl.ds(items[0][0], len(items))
        send(margin_out.at[side, block, which], margin_in.at[1 - side, block, which],
             send_far.at[k // DEPTH, side, block], recv_far.at[k // DEPTH, 1 - side, block], side, go)

    def halo_arrived(k, block):
        for side in range(2):
            @pl.when(has_low if side == 0 else has_high)
            def _():
                where = pl.ds(0 if side == 0 else layers + DEPTH, DEPTH)
                if k == 0:
                    arrived(fields.at[k, where, block], recv_halo.at[k // DEPTH, side, block])
                    return
                items = margin_items(k, side, False)
                which = pl.ds(items[0][0], len(items))
                arrived(fields.at[k, where, block, :, inside], recv_halo.at[k // DEPTH, side, block])
                arrived(margin_in.at[side, block, which], recv_far.at[k // DEPTH, side, block])
                for item, at in items:
                    @pl.when(inside_at >= 8)
                    def _():
                        fields[k, at, block, :, tile_low] = margin_in[side, block, item]

                    @pl.when(inside_at + part <= window - 8)
                    def _():
                        fields[k, at, block, :, tile_high] = margin_in[side, block, item]

    def near(ref, index, side, go):
        send(ref.at[1 if side == 0 else layers], ref.at[layers + 1 if side == 0 else 0],
             send_near.at[index, side], recv_near.at[index, 1 - side], side, go)

    def near_arrived(ref, index):
        for side in range(2):
            @pl.when(has_low if side == 0 else has_high)
            def _():
                arrived(ref.at[0 if side == 0 else layers + 1], recv_near.at[index, side])

    def scaled(f, layer):
        shift_re, shift_im = shift_in[f, 0:1], shift_in[f, 1:2]
        back_re, back_im = back_in[f, 0, layer], back_in[f, 1, layer]
        return shift_re * back_re - shift_im * back_im, shift_re * back_im + shift_im * back_re

    def invert(f, index):
        shift_re, shift_im = shift_in[f, 0:1], shift_in[f, 1:2]
        medium = medium_in[index]
        diag_re = 6.0 + shift_re * medium
        diag_im = shift_im * medium
        scale = OMEGA_RELAX / (diag_re * diag_re + diag_im * diag_im)
        inv_re = diag_re * scale
        inv_im = -diag_im * scale
        inverse[f, 0, index] = inv_re
        inverse[f, 1, index] = inv_im
        return inv_re, inv_im

    order = list(range(DEPTH)) + [i for i in range(layers - DEPTH, layers) if i >= DEPTH]
    order += [i for i in range(layers) if i not in order]
    ready_low, ready_high = DEPTH, min(2 * DEPTH, layers)

    for owner in range(2):
        arrived(medium_in.at[pl.ds(1 + owner * own, own)], recv_medium.at[owner])
    for side in range(2):
        near(medium_in, 0, side, True)

    def first(turn):
        f = lax.rem(h + turn, freqs)

        @pl.when(turn != 0)
        def _():
            arrived(shift_in.at[f], recv_shift.at[f])

        for owner in range(2):
            arrived(back_in.at[f, :, pl.ds(owner * own, own)], recv_back.at[f, owner])

        for p in range(num_probes):
            block = f * num_probes + p

            @pl.when(turn == 0)
            def _():
                for owner in range(2):
                    arrived(probes_in.at[p, pl.ds(owner * own, own)], recv_probes.at[p, owner])

            for done, layer in enumerate(order):
                if p == 0:
                    inv_re, inv_im = invert(f, 1 + layer)
                    scaled_re, scaled_im = scaled(f, layer)
                    start[0, layer] = inv_re * scaled_re - inv_im * scaled_im
                    start[1, layer] = inv_re * scaled_im + inv_im * scaled_re
                probe = probes_in[p, layer]
                fields[0, DEPTH + layer, block, 0] = start[0, layer] * probe
                fields[0, DEPTH + layer, block, 1] = start[1, layer] * probe
                if done + 1 == ready_low:
                    halo(0, block, 0, True)
                if done + 1 == ready_high:
                    halo(0, block, 1, True)

    first(0)
    for owner in range(2):
        arrived(listen_in.at[pl.ds(1 + owner * own, own)], recv_listen.at[owner])
    for side in range(2):
        near(listen_in, 1, side, True)
    pl.loop(1, freqs)(first)

    def update(k, f, block, at, sign):
        new = []
        for part_of in range(2):
            beside = fields[k, at - 1, block, part_of] + fields[k, at + 1, block, part_of]
            new.append(beside + spread(fields[k, at, block, part_of]))
        sum_re, sum_im = new
        inv_re = inverse[f, 0, at - 1]
        inv_im = sign * inverse[f, 1, at - 1]
        origin = 0 if k < STEPS - 1 else STEPS - 1
        keep = 1.0 - OMEGA_RELAX
        next_re = keep * fields[k, at, block, 0] + fields[origin, at, block, 0]
        next_im = keep * fields[k, at, block, 1] + fields[origin, at, block, 1]
        next_re = next_re + (inv_re * sum_re - inv_im * sum_im)
        next_im = next_im + (inv_re * sum_im + inv_im * sum_re)
        return next_re, next_im

    def advance(k, f, block, at):
        next_re, next_im = update(k, f, block, at, 1.0 if k < STEPS - 1 else -1.0)
        if k == STEPS - 2:
            listen = listen_in[at - 1].astype(jnp.float32)
            next_re = next_re * listen
            next_im = next_im * listen
            inv_re, inv_im = inverse[f, 0, at - 1], inverse[f, 1, at - 1]
            next_re, next_im = (
                inv_re * next_re + inv_im * next_im,
                inv_re * next_im - inv_im * next_re,
            )
        fields[k + 1, at, block, 0] = next_re
        fields[k + 1, at, block, 1] = next_im

    def invert_near(f):
        for side in range(2):
            there = has_low if side == 0 else has_high
            index = 0 if side == 0 else layers + 1

            @pl.when(there)
            def _():
                invert(f, index)

            @pl.when(jnp.logical_not(there))
            def _():
                inverse[f, :, index] = jnp.zeros_like(inverse[f, :, index])

    for k in sent[:-1]:
        if k == 0:
            near_arrived(medium_in, 0)
        if k == DEPTH:
            near_arrived(listen_in, 1)

        @pl.loop(0, freqs)
        def _(turn, k=k):
            f = lax.rem(h + turn, freqs)
            if k == 0:
                invert_near(f)
            for p in range(num_probes):
                block = f * num_probes + p
                halo_arrived(k, block)
                for at in range(1, layers + 3):
                    advance(k, f, block, at)
                for done, layer in enumerate(order):
                    advance(k + 1, f, block, DEPTH + layer)
                    if done + 1 == ready_low:
                        halo(k + DEPTH, block, 0, True)
                    if done + 1 == ready_high:
                        halo(k + DEPTH, block, 1, True)

    def send_terms(p, go):
        for owner in range(2):
            put(terms.at[p, pl.ds(owner * own, own), inside],
                out_ref.at[p, :, pl.ds(pl.multiple_of(q * part, 8), part)],
                send_out.at[p, owner], recv_out.at[p, q], h, base + 2 * c + owner, go)

    def add_terms(f, p, start):
        block = f * num_probes + p
        halo_arrived(last - 1, block)
        for at in range(1, layers + 3):
            advance(last - 1, f, block, at)
        for layer in range(layers):
            scaled_re, scaled_im = scaled(f, layer)
            next_re, next_im = update(last, f, block, DEPTH + layer, -1.0)
            term = scaled_re * next_re + scaled_im * next_im
            terms[p, layer] = term if start else terms[p, layer] + term

    for p in range(num_probes):
        add_terms(h, p, True)

    if freqs > 2:
        @pl.loop(1, freqs - 1)
        def _(turn):
            for p in range(num_probes):
                add_terms(lax.rem(h + turn, freqs), p, False)

    for p in range(num_probes):
        if freqs > 1:
            add_terms(lax.rem(h + freqs - 1, freqs), p, False)
        send_terms(p, True)

    for p in range(num_probes):
        for pair in range(PAIRS):
            arrived(out_ref.at[p, :, pl.ds(pair * part, part)], recv_out.at[p, pair])
    for p in range(num_probes):
        send_terms(p, False)
    send_inputs(False)
    for side in range(2):
        near(medium_in, 0, side, False)
        near(listen_in, 1, side, False)
    for k in sent:
        @pl.loop(0, freqs * num_probes)
        def _(block, k=k):
            halo(k, block, 0, False)
            halo(k, block, 1, False)


def per_device(freqs, spaces, probes, background, medium, shifts, receivers):
    num_probes, own, rows_all, lanes = probes.shape
    layers = PAIRS * own
    part = rows_all // (freqs * PAIRS)
    window = part + 2 * MARGIN
    blocks = freqs * num_probes
    count = 2 * (STEPS - 1)
    dma = pltpu.SemaphoreType.DMA
    any_spec = pl.BlockSpec(memory_space=pl.ANY)
    return pl.pallas_call(
        functools.partial(kernel, freqs, spaces, rows_all),
        out_shape=jax.ShapeDtypeStruct((num_probes, own, rows_all // freqs, lanes), jnp.float32),
        in_specs=[pl.BlockSpec(memory_space=pltpu.SMEM)] + [any_spec] * 4,
        out_specs=any_spec,
        scratch_shapes=[
            pltpu.VMEM((num_probes, layers, window, lanes), jnp.float32),
            pltpu.VMEM((freqs, 2, layers, window, lanes), jnp.float32),
            pltpu.VMEM((layers + 2, window, lanes), jnp.float32),
            pltpu.VMEM((layers + 2, window, lanes), jnp.int32),
            pltpu.VMEM((8, lanes), jnp.float32),
            pltpu.VMEM((freqs, 8, lanes), jnp.float32),
            pltpu.VMEM((freqs, 2, layers + 2, window, lanes), jnp.float32),
            pltpu.VMEM((2, layers, window, lanes), jnp.float32),
            pltpu.VMEM((2, blocks, 3, 2, 8, lanes), jnp.float32),
            pltpu.VMEM((2, blocks, 3, 2, 8, lanes), jnp.float32),
            pltpu.VMEM((count, layers + 2 * DEPTH, blocks, 2, window, lanes), jnp.float32),
            pltpu.VMEM((num_probes, layers, window, lanes), jnp.float32),
            dma((2 + num_probes, PAIRS)),
            dma((num_probes, 2)),
            dma((2,)),
            dma((2,)),
            dma((freqs, 2)),
            dma((freqs, PAIRS)),
            dma((freqs,)),
            dma((freqs,)),
            dma((count // DEPTH, 2, blocks)),
            dma((count // DEPTH, 2, blocks)),
            dma((count // DEPTH, 2, blocks)),
            dma((count // DEPTH, 2, blocks)),
            dma((2, 2)),
            dma((2, 2)),
            dma((num_probes, 2)),
            dma((num_probes, PAIRS)),
        ],
        compiler_params=pltpu.CompilerParams(collective_id=0, has_side_effects=True),
    )(shifts, probes, background, medium, receivers)


def solution(mesh):
    in_specs = (
        P(None, "space", None, None),
        P("freq", None, "space", None, None),
        P("space", None, None),
        P("freq", None),
        P("space", None, None),
    )
    out_specs = P(None, "space", "freq", None)
    return jax.shard_map(
        functools.partial(per_device, mesh.shape["freq"], mesh.shape["space"]),
        mesh=mesh, in_specs=in_specs, out_specs=out_specs, check_vma=False,
    )
```
